32 devices in a mesh: pos: 8 (over z, core), mode: 4 (over y, x).
Axes of the slice: x: 2, y: 2, z: 4, core: 2. Of those that a mesh axis runs over, the one named last changes fastest.
Arguments:
- grid_input: bfloat16 [8, 128, 32, 256], P('mode', 'pos'), may hold values from -6 to 6
- preact: bfloat16 [8, 128, 32, 256], P('mode', 'pos'), may hold values from -6 to 6
- out_grad: bfloat16 [8, 128, 32, 256], P('mode', 'pos'), may hold values from -6 to 6
- mode_weight: bfloat16 [2, 64, 32, 256, 256], P(None, 'mode', 'pos'), may hold values from -0.375 to 0.375
- local_weight: bfloat16 [256, 256], replicated, may hold values from -0.375 to 0.375
Outputs:
- grad_input: bfloat16 [8, 128, 32, 256], P('mode', 'pos')
- grad_modes: bfloat16 [2, 64, 32, 256, 256], P(None, 'mode', 'pos')
The draws below stay inside these ranges and needn't reach their ends.
All inputs are finite; a program needn't handle non-finite values.
Results may differ from the reference program's by a relative error of at most 0.0087.
Values may be sent and summed in bfloat16 or wider, within the bound.
A program may use at most 128 MiB of HBM per device.

```python
import math
import jax
import jax.numpy as jnp
from jax import lax

C = 256
KA = 64
KT = 32
NT = 32
B = 8
NA = 128


def block_scale(own_key, dims, pieces, smallest, high):
    level, own = 1.0, jax.random.fold_in(own_key, 6)
    for axis_at, parts in pieces:
        steps = jnp.exp(jax.random.uniform(jax.random.fold_in(own, axis_at), (parts,), jnp.float32, smallest / len(pieces), high / len(pieces)))
        level = level * jnp.repeat(steps, dims[axis_at] // parts).reshape([-1 if axis == axis_at else 1 for axis in range(len(dims))])
    return level


def centred(key, shape, width, bound, shards=(), kind=jnp.bfloat16):
    drawn = width * jax.random.normal(key, shape, jnp.float32)
    if shards:
        drawn = drawn * block_scale(key, shape, shards, -0.22, 0.18)
    return jnp.clip(drawn, -bound, bound).astype(kind)


def setup_inputs(seed: int = 0) -> dict:
    arg_keys = jax.random.split(jax.random.key(seed), 6)
    return {
        "grid_input": centred(arg_keys[0], (B, NA, NT, C), 1.0, 6.0, ((0, 4), (1, 8))),
        "preact": centred(arg_keys[1], (B, NA, NT, C), 1.0, 6.0, ((0, 4), (1, 8))),
        "out_grad": centred(arg_keys[2], (B, NA, NT, C), 1.0, 6.0, ((0, 4), (1, 8))),
        "mode_weight": centred(arg_keys[3], (2, KA, KT, C, C), C ** -0.5, 0.375, ((1, 4), (2, 8))),
        "local_weight": centred(arg_keys[4], (C, C), C ** -0.5, 0.375),
    }


def twiddle(length, mode_count):
    product = (jnp.arange(length).astype(jnp.int32)[:, None] * jnp.arange(mode_count).astype(jnp.int32)[None, :]) % length
    angles = product.astype(jnp.float32) * (2.0 * math.pi / length)
    return jnp.cos(angles).astype(jnp.bfloat16), jnp.sin(angles).astype(jnp.bfloat16)


def gelu_slope(preact, out_grad):
    values = preact.astype(jnp.float32)
    normal_cdf = 0.5 * (1.0 + lax.erf(values * 0.7071067811865476))
    density = jnp.exp(-0.5 * values * values) * 0.3989422804014327
    return (out_grad.astype(jnp.float32) * (normal_cdf + values * density)).astype(jnp.bfloat16)


def time_forward(field_in, cos_time, sin_time):
    field_wide = field_in.astype(jnp.float32)
    real_part = jnp.einsum('batc,tk->bakc', field_wide, cos_time.astype(jnp.float32))
    imag_part = -jnp.einsum('batc,tk->bakc', field_wide, sin_time.astype(jnp.float32))
    return real_part.astype(jnp.bfloat16), imag_part.astype(jnp.bfloat16)


def space_forward(real_in, imag_in, cos_space, sin_space, factor):
    real_wide = real_in.astype(jnp.float32)
    imag_wide = imag_in.astype(jnp.float32)
    cos_wide = cos_space.astype(jnp.float32)
    sin_wide = sin_space.astype(jnp.float32)
    real_out = jnp.einsum('bakc,aq->bqkc', real_wide, cos_wide) + jnp.einsum('bakc,aq->bqkc', imag_wide, sin_wide)
    imag_out = jnp.einsum('bakc,aq->bqkc', imag_wide, cos_wide) - jnp.einsum('bakc,aq->bqkc', real_wide, sin_wide)
    return (real_out * factor).astype(jnp.bfloat16), (imag_out * factor).astype(jnp.bfloat16)


def per_mode(operands):
    input_real, input_imaginary, upstream_real, upstream_imaginary, weight = operands
    input_real = input_real.astype(jnp.float32)
    input_imaginary = input_imaginary.astype(jnp.float32)
    upstream_real = upstream_real.astype(jnp.float32)
    upstream_imaginary = upstream_imaginary.astype(jnp.float32)
    weight_real = weight[0].astype(jnp.float32)
    weight_imaginary = weight[1].astype(jnp.float32)
    gradient_real = jnp.einsum('szx,szr->zxr', input_real, upstream_real) + jnp.einsum('szx,szr->zxr', input_imaginary, upstream_imaginary)
    gradient_imaginary = jnp.einsum('szx,szr->zxr', input_real, upstream_imaginary) - jnp.einsum('szx,szr->zxr', input_imaginary, upstream_real)
    backward_real = jnp.einsum('erl,ril->eri', upstream_real, weight_real) + jnp.einsum('erl,ril->eri', upstream_imaginary, weight_imaginary)
    backward_imaginary = jnp.einsum('erl,ril->eri', upstream_imaginary, weight_real) - jnp.einsum('erl,ril->eri', upstream_real, weight_imaginary)
    return jnp.stack([gradient_real, gradient_imaginary]).astype(jnp.bfloat16), jnp.stack([backward_real, backward_imaginary]).astype(jnp.bfloat16)


def reference(grid_input, preact, out_grad, mode_weight, local_weight):
    cos_time, sin_time = twiddle(NT, KT)
    cos_space, sin_space = twiddle(NA, KA)
    slope = gelu_slope(preact, out_grad)
    x_tr, x_ti = time_forward(grid_input, cos_time, sin_time)
    input_real, input_imaginary = space_forward(x_tr, x_ti, cos_space, sin_space, 1.0)
    g_tr, g_ti = time_forward(slope, cos_time, sin_time)
    upstream_real, upstream_imaginary = space_forward(g_tr, g_ti, cos_space, sin_space, 1.0 / (NA * NT))
    order = (1, 0, 2, 3)
    grads, backs = lax.map(per_mode, (jnp.transpose(input_real, order), jnp.transpose(input_imaginary, order), jnp.transpose(upstream_real, order), jnp.transpose(upstream_imaginary, order), jnp.transpose(mode_weight, (1, 0, 2, 3, 4))))
    grad_modes = jnp.transpose(grads, (1, 0, 2, 3, 4))
    backs = jnp.transpose(backs, (1, 2, 0, 3, 4))
    backward_real = backs[0].astype(jnp.float32)
    backward_imaginary = backs[1].astype(jnp.float32)
    cos_wide = cos_space.astype(jnp.float32)
    sin_wide = sin_space.astype(jnp.float32)
    spread_real = (jnp.einsum('bqkc,aq->bakc', backward_real, cos_wide) - jnp.einsum('bqkc,aq->bakc', backward_imaginary, sin_wide)).astype(jnp.bfloat16)
    spread_imag = (jnp.einsum('bqkc,aq->bakc', backward_real, sin_wide) + jnp.einsum('bqkc,aq->bakc', backward_imaginary, cos_wide)).astype(jnp.bfloat16)
    spectral = jnp.einsum('bakc,tk->batc', spread_real.astype(jnp.float32), cos_time.astype(jnp.float32)) - jnp.einsum('bakc,tk->batc', spread_imag.astype(jnp.float32), sin_time.astype(jnp.float32))
    local_term = jnp.dot(slope.reshape(-1, C), local_weight.T, preferred_element_type=jnp.float32)
    grad_input = (spectral + local_term.reshape(spectral.shape)).astype(jnp.bfloat16)
    return grad_input, grad_modes
```

```python
import functools
import math

import jax
import jax.numpy as jnp
import ml_dtypes
import numpy as np
from jax import lax
from jax.experimental import pallas as pl
from jax.experimental.pallas import tpu as pltpu
from jax.sharding import PartitionSpec as P

MESH = pl.DeviceIdType.MESH
F32 = jnp.float32
BF16 = jnp.bfloat16
GROUP = 128


def twiddle(length, mode_count):
    angles = (np.arange(length)[:, None] * np.arange(mode_count)[None, :] % length) * (2.0 * math.pi / length)
    as_bf16 = lambda v: v.astype(np.float32).astype(ml_dtypes.bfloat16).astype(np.float32)
    return as_bf16(np.cos(angles)), as_bf16(np.sin(angles))


def tables(np_, nm, nb, na, nt, nk, nq):
    cos_t, sin_t = twiddle(nt, np_ * nk)
    cos_s, sin_s = twiddle(np_ * na, nm * nq)
    eye_a, eye_b, eye_m, eye_q = np.eye(na), np.eye(nb), np.eye(nm), np.eye(nq)
    out = lambda v, *shape: jnp.asarray(v.reshape(shape).astype(ml_dtypes.bfloat16))
    by_k = np.stack([cos_t, -sin_t])
    by_k = by_k.reshape(2, nt, np_, nk)
    time_fwd = np.einsum("rtpk,ab->kprabt", by_k, eye_a)
    time_far = np.einsum("rtpk,ab->patkrb", by_k, eye_a)
    fwd = np.stack([np.stack([cos_s, sin_s]), np.stack([-sin_s, cos_s])])
    fwd = fwd.reshape(2, 2, np_, na, nm, nq)
    space_fwd = np.einsum("rspamq,bc->mbrqpcsa", fwd, eye_b)
    pick = np.einsum("rs,qu,mn,bc->qrmbncsu", np.eye(2), eye_q, eye_m, eye_b)
    turn = np.einsum("rs,qu,mn,bc->qrmbncsu", np.array([[0.0, 1.0], [-1.0, 0.0]]), eye_q, eye_m, eye_b)
    rows = nm * nb * 2 * nq
    return (
        out(time_fwd, nk, np_ * 2 * na, na * nt),
        out(space_fwd, rows, np_ * nb * 2 * na),
        out(pick, rows, rows),
        out(turn, rows, rows),
        out(time_far, np_, na * nt, nk * 2 * na),
    )


def dot(a, b):
    return jnp.dot(a, b, preferred_element_type=F32)


def dot_t(a, b):
    return lax.dot_general(a, b, (((1,), (1,)), ((), ())), preferred_element_type=F32)


def chain_kernel(
    np_, nm, factor,
    pre_hbm, og_hbm, tf_hbm, x_hbm, sf_hbm, pick_hbm, turn_hbm, lw_hbm, w_hbm,
    acc, far_hbm, xo_ref, g1_ref, g2_ref,
    pre_ref, og_ref, tf_ref, x_ref, sf_ref, pick_ref, turn_ref, lw_ref, w_buf, unpick_ref, si_ref, ti_ref,
    slope, gs, gr, xs, xr, ms, mr, ns, nr, bk, bs, br, ts, tr,
    in_sem, tf_sem, far_sem, g_ss, g_rs, x_ss, x_rs, m_ss, m_rs, n_ss, n_rs, b_ss, b_rs, t_ss, t_rs,
):
    nb, rows, c = slope.shape
    _, nk, _, ra, _ = gs.shape
    nq = w_buf.shape[1]
    unit = bk.shape[1] // nq
    pos, mode = lax.axis_index("pos"), lax.axis_index("mode")
    at = {"pos": pos, "mode": mode}
    size = {"pos": np_, "mode": nm}
    peer_of = lambda axis, d: lax.rem(at[axis] + d, size[axis])

    barrier = pltpu.get_barrier_semaphore()
    for axis in ("pos", "mode"):
        for d in range(1, size[axis]):
            pl.semaphore_signal(barrier, inc=1, device_id={axis: peer_of(axis, d)}, device_id_type=MESH)

    far = lax.rem(pos + np_ // 2, np_)
    hbm = (x_hbm, pre_hbm, og_hbm, sf_hbm, pick_hbm, turn_hbm, lw_hbm, w_hbm)
    local = (x_ref, pre_ref, og_ref, sf_ref, pick_ref, turn_ref, lw_ref, w_buf)
    loads = [pltpu.make_async_copy(h, v, in_sem.at[n]) for n, (h, v) in enumerate(zip(hbm, local))]
    tf_loads = [pltpu.make_async_copy(tf_hbm.at[k], tf_ref.at[k], tf_sem.at[k]) for k in range(nk)]
    for load in (loads[0], tf_loads[0], *loads[1:3], *tf_loads[1:], *loads[3:]):
        load.start()
    load_of = {id(v): load for v, load in zip(local, loads)}
    ready = lambda *refs: [load_of[id(r)].wait() for r in refs]

    step = 64

    def slope_step(i):
        b, r = i // (rows // step), pl.multiple_of(i % (rows // step) * step, step)
        values = pre_ref[b, pl.ds(r, step), :].astype(F32)
        cdf = 0.5 * (1.0 + lax.erf(values * 0.7071067811865476))
        density = jnp.exp(-0.5 * values * values) * 0.3989422804014327
        grad = og_ref[b, pl.ds(r, step), :].astype(F32)
        slope[b, pl.ds(r, step), :] = (grad * (cdf + values * density)).astype(BF16)

    def copy(axis, peer, slot, k, src, dst, ss, rs):
        return pltpu.make_async_remote_copy(
            src_ref=src.at[peer, k], dst_ref=dst.at[slot, k], send_sem=ss.at[peer, k], recv_sem=rs.at[slot, k],
            device_id={axis: peer}, device_id_type=MESH,
        )

    def peers(axis, skip, act):
        half = size[axis] // 2
        for first, last in ((1, half), (half + 1, size[axis])) if skip else ((1, size[axis]),):
            if first < last:
                pl.loop(first, last)(lambda d: act(peer_of(axis, d)))

    def send(axis, k, src, dst, ss, rs, skip=False):
        peers(axis, skip, lambda peer: copy(axis, peer, at[axis], k, src, dst, ss, rs).start())
        dst[at[axis], k] = src[at[axis], k]

    def arrive(axis, k, src, dst, ss, rs, skip=False):
        peers(axis, skip, lambda peer: copy(axis, peer, peer, k, src, dst, ss, rs).wait_recv())

    def drain(axis, k, src, dst, ss, rs, skip=False):
        peers(axis, skip, lambda peer: copy(axis, peer, peer, k, src, dst, ss, rs).wait_send())

    g_way = ("pos", gs, gr, g_ss, g_rs)
    x_way = ("pos", xs, xr, x_ss, x_rs)
    m_way = ("mode", ms, mr, m_ss, m_rs)
    n_way = ("mode", ns, nr, n_ss, n_rs)
    b_way = ("mode", bs, br, b_ss, b_rs)
    t_way = ("pos", ts, tr, t_ss, t_rs, True)
    go = lambda act, k, way: act(way[0], k, *way[1:])

    def time_fwd(source, buf, k):
        for b in range(nb):
            buf[:, k, b] = dot(tf_ref[k], source[b]).astype(BF16).reshape(np_, ra, c)

    def space_fwd(source, buf, k, scale):
        res = dot(sf_ref[...], source[:, k].reshape(-1, c))
        if scale != 1.0:
            res = res * scale
        buf[:, k] = res.astype(BF16).reshape(nm, -1, c)

    def gathered(buf, k):
        return buf[:, k].reshape(-1, c)

    ready(x_ref)
    tf_loads[0].wait()
    time_fwd(x_ref, xs, 0)
    pl.semaphore_wait(barrier, np_ - 1 + nm - 1)
    go(send, 0, x_way)
    ready(pre_ref, og_ref)
    pl.loop(0, nb * (rows // step))(slope_step)
    for k in range(nk):
        if k:
            tf_loads[k].wait()
        time_fwd(slope, gs, k)
        go(send, k, g_way)
    for k in range(1, nk):
        time_fwd(x_ref, xs, k)
    tr[far] = jnp.zeros(tr.shape[1:], BF16)
    ready(sf_ref, pick_ref, turn_ref, lw_ref, w_buf)
    unpick_ref[...] = pick_ref[...].T
    si_ref[...] = sf_ref[...].T
    for k in range(nk):
        ti_ref[k] = tf_ref[k].T

    far_copy = lambda k: pltpu.make_async_copy(ts.at[far, k], far_hbm.at[:, k], far_sem.at[k])

    def stage_space(k):
        go(arrive, k, g_way)
        go(drain, k, g_way)
        if k + 1 < nk:
            go(send, k + 1, x_way)
        space_fwd(gr, ms, k, factor)
        go(send, k, m_way)

    def stage_back(k):
        go(arrive, k, m_way)
        field = gathered(mr, k)
        g1_ref[k] = dot(pick_ref[...], field).astype(BF16)
        g2_ref[k] = dot(turn_ref[...], field).astype(BF16)

        @pl.loop(0, nq, unroll=math.gcd(nq, 4))
        def _(q):
            span = pl.ds(pl.multiple_of(q * unit, unit), unit)
            back = dot_t(g1_ref[k, span, :], w_buf[0, q, k]) + dot_t(g2_ref[k, span, :], w_buf[1, q, k])
            bk[k, span, :] = back.astype(BF16)

        bs[:, k] = dot(unpick_ref[...], bk[k]).astype(BF16).reshape(nm, -1, c)
        go(send, k, b_way)

    def stage_spread(k):
        go(arrive, k, b_way)
        spread = dot(si_ref[...], gathered(br, k)).astype(BF16)
        ts[:, k] = spread.reshape(np_, nb, ra, c)
        go(send, k, t_way)
        far_copy(k).start()

    def stage_x(k):
        go(arrive, k, x_way)
        space_fwd(xr, ns, k, 1.0)
        go(send, k, n_way)

    def stage_own(k):
        go(arrive, k, n_way)
        xo_ref[k] = dot(pick_ref[...], gathered(nr, k)).astype(BF16)

    def staged(*stages):
        for n in range(nk + len(stages) - 1):
            for lag, stage in enumerate(stages):
                if 0 <= n - lag < nk:
                    stage(n - lag)

    staged(stage_space, stage_back, stage_spread)
    for b in range(nb):
        acc[b] = dot_t(slope[b], lw_ref[...])
    staged(stage_x, stage_own)
    for k in range(nk):
        for way in (x_way, m_way, n_way, b_way):
            go(drain, k, way)

    for k in range(nk):
        go(arrive, k, t_way)
        for b in range(nb):
            acc[b] = acc[b] + dot(ti_ref[k], tr[:, k, b].reshape(-1, c))
    for k in range(nk):
        go(drain, k, t_way)
        far_copy(k).wait()


def modes_kernel(group, x_ref, g1_ref, g2_ref, out_hbm, buf, sem):
    nk, nq, unit, c = x_ref.shape

    @pl.loop(0, nk)
    def _(k):
        @pl.loop(0, nq // group)
        def _(i):
            first = i * group
            turned = x_ref[k, pl.ds(first, group)].reshape(group * unit, c).T
            for q in range(group):
                for part, g_ref in enumerate((g1_ref, g2_ref)):
                    rows = [jnp.zeros((n * unit, c), BF16) if n else None for n in (q, group - 1 - q)]
                    rows = [v for v in (rows[0], g_ref[k, first + q], rows[1]) if v is not None]
                    field = jnp.concatenate(rows, axis=0) if len(rows) > 1 else rows[0]
                    buf[part, first + q, k] = dot(turned, field).astype(BF16)
                    pltpu.make_async_copy(buf.at[part, first + q, k], out_hbm.at[part, first + q, k], sem).start()

    pltpu.make_async_copy(buf, out_hbm, sem).wait()


def finish_kernel(np_, acc_ref, far_ref, tab_hbm, out_hbm, tab_ref, out_ref, in_sem, out_sem):
    nb = acc_ref.shape[0]
    peer = lax.rem(lax.axis_index("pos") + np_ // 2, np_)
    tab = pltpu.make_async_copy(tab_hbm.at[peer], tab_ref, in_sem)
    outs = [pltpu.make_async_copy(out_ref.at[b], out_hbm.at[b], out_sem.at[b]) for b in range(nb)]
    tab.start()
    tab.wait()
    for b in range(nb):
        out_ref[b] = (acc_ref[b] + dot(tab_ref[...], far_ref[b])).astype(BF16)
        outs[b].start()
    for b in range(nb):
        outs[b].wait()


def on_device(np_, nm, grid_input, preact, out_grad, mode_weight, local_weight):
    nb, na, nt, c = grid_input.shape
    _, nq, nk, _, _ = mode_weight.shape
    factor = 1.0 / (np_ * na * nt)
    consts = tables(np_, nm, nb, na, nt, nk, nq)
    unit = nm * nb * 2
    flat = lambda v: v.reshape(nb, na * nt, c)
    operands = (
        flat(preact), flat(out_grad), consts[0], flat(grid_input), *consts[1:-1], local_weight, mode_weight
    )
    anywhere = pl.BlockSpec(memory_space=pl.ANY)
    on_chip = pl.BlockSpec(memory_space=pltpu.VMEM)
    in_place = pl.BlockSpec(memory_space=pltpu.HBM)
    pos_buf = pltpu.VMEM((np_, nk, nb, 2 * na, c), BF16)
    mode_buf = pltpu.VMEM((nm, nk, nb * 2 * nq, c), BF16)
    owned = jax.ShapeDtypeStruct((nk, nq * unit, c), BF16)
    field = jax.ShapeDtypeStruct((nb, na * nt, c), BF16)
    total = jax.ShapeDtypeStruct(field.shape, F32)
    far = jax.ShapeDtypeStruct((nb, nk, 2 * na, c), BF16)
    dma = pltpu.SemaphoreType.DMA
    sems = [dma((n, nk)) for n in (np_, np_, np_, np_, nm, nm, nm, nm, nm, nm, np_, np_)]
    acc, far, x_own, g1, g2 = pl.pallas_call(
        functools.partial(chain_kernel, np_, nm, factor),
        out_shape=(total, far, owned, owned, owned),
        in_specs=[in_place] * len(operands),
        out_specs=(on_chip, anywhere, on_chip, on_chip, on_chip),
        scratch_shapes=[pltpu.VMEM(v.shape, BF16) for v in operands]
        + [
            pltpu.VMEM(consts[2].shape, BF16),
            pltpu.VMEM(consts[1].shape[::-1], BF16),
            pltpu.VMEM((nk, na * nt, np_ * 2 * na), BF16),
            pltpu.VMEM(field.shape, BF16),
            pos_buf, pos_buf, pos_buf, pos_buf,
            mode_buf, mode_buf, mode_buf, mode_buf,
            pltpu.VMEM(owned.shape, BF16),
            mode_buf, mode_buf,
            pos_buf, pos_buf,
            dma((len(operands),)), dma((nk,)), dma((nk,)),
        ] + sems,
        compiler_params=pltpu.CompilerParams(
            collective_id=0, has_side_effects=True, vmem_limit_bytes=40 * 1024 * 1024
        ),
        name="chain",
    )(*[pltpu.with_memory_space_constraint(v, pltpu.HBM) for v in operands])

    far = lax.ppermute(far, "pos", [(n, (n + np_ // 2) % np_) for n in range(np_)])
    per_q = lambda v: v.reshape(nk, nq, unit, c)
    group = max(n for n in range(1, nq + 1) if nq % n == 0 and n * unit <= max(GROUP, unit))
    grad_modes = pl.pallas_call(
        functools.partial(modes_kernel, group),
        out_shape=jax.ShapeDtypeStruct(mode_weight.shape, BF16),
        in_specs=[on_chip] * 3,
        out_specs=anywhere,
        scratch_shapes=[pltpu.VMEM(mode_weight.shape, BF16), dma(())],
        cost_estimate=pl.CostEstimate(
            flops=2 * unit * mode_weight.size, bytes_accessed=2 * mode_weight.size, transcendentals=0
        ),
        compiler_params=pltpu.CompilerParams(vmem_limit_bytes=24 * 1024 * 1024),
        name="modes",
    )(per_q(x_own), per_q(g1), per_q(g2))
    grad_input = pl.pallas_call(
        functools.partial(finish_kernel, np_),
        out_shape=field,
        in_specs=[on_chip, on_chip, in_place],
        out_specs=anywhere,
        scratch_shapes=[
            pltpu.VMEM(consts[-1].shape[1:], BF16),
            pltpu.VMEM(field.shape, BF16),
            dma(()), dma((nb,)),
        ],
        compiler_params=pltpu.CompilerParams(vmem_limit_bytes=16 * 1024 * 1024),
        name="finish",
    )(acc, far.reshape(nb, nk * 2 * na, c), consts[-1])
    return (grad_input.reshape(grid_input.shape), grad_modes)


def solution(mesh):
    return jax.shard_map(
        functools.partial(on_device, mesh.shape["pos"], mesh.shape["mode"]),
        mesh=mesh,
        in_specs=(
            P("mode", "pos", None, None),
            P("mode", "pos", None, None),
            P("mode", "pos", None, None),
            P(None, "mode", "pos", None, None),
            P(),
        ),
        out_specs=(P("mode", "pos", None, None), P(None, "mode", "pos", None, None)),
        check_vma=False,
    )
```

```python
import functools
import math

import jax
import jax.numpy as jnp
import ml_dtypes
import numpy as np
from jax import lax
from jax.experimental import pallas as pl
from jax.experimental.pallas import tpu as pltpu
from jax.sharding import PartitionSpec as P

MESH = pl.DeviceIdType.MESH
F32 = jnp.float32
BF16 = jnp.bfloat16
GROUP = 128


def twiddle(length, mode_count):
    angles = (np.arange(length)[:, None] * np.arange(mode_count)[None, :] % length) * (2.0 * math.pi / length)
    as_bf16 = lambda v: v.astype(np.float32).astype(ml_dtypes.bfloat16).astype(np.float32)
    return as_bf16(np.cos(angles)), as_bf16(np.sin(angles))


def tables(np_, nm, nb, na, nt, nk, nq):
    cos_t, sin_t = twiddle(nt, np_ * nk)
    cos_s, sin_s = twiddle(np_ * na, nm * nq)
    eye_a, eye_b, eye_m, eye_q = np.eye(na), np.eye(nb), np.eye(nm), np.eye(nq)
    out = lambda v, *shape: jnp.asarray(v.reshape(shape).astype(ml_dtypes.bfloat16))
    by_k = np.stack([cos_t, -sin_t])
    by_k = by_k.reshape(2, nt, np_, nk)
    time_fwd = np.einsum("rtpk,ab->kprabt", by_k, eye_a)
    time_far = np.einsum("rtpk,ab->patkrb", by_k, eye_a)
    fwd = np.stack([np.stack([cos_s, sin_s]), np.stack([-sin_s, cos_s])])
    fwd = fwd.reshape(2, 2, np_, na, nm, nq)
    space_fwd = np.einsum("rspamq,bc->mbrqpcsa", fwd, eye_b)
    pick = np.einsum("rs,qu,mn,bc->qrmbncsu", np.eye(2), eye_q, eye_m, eye_b)
    turn = np.einsum("rs,qu,mn,bc->qrmbncsu", np.array([[0.0, 1.0], [-1.0, 0.0]]), eye_q, eye_m, eye_b)
    rows = nm * nb * 2 * nq
    return (
        out(time_fwd, nk, np_ * 2 * na, na * nt),
        out(space_fwd, rows, np_ * nb * 2 * na),
        out(pick, rows, rows),
        out(turn, rows, rows),
        out(time_far, np_, na * nt, nk * 2 * na),
    )


def dot(a, b):
    return jnp.dot(a, b, preferred_element_type=F32)


def dot_t(a, b):
    return lax.dot_general(a, b, (((1,), (1,)), ((), ())), preferred_element_type=F32)


def chain_kernel(
    np_, nm, factor,
    pre_hbm, og_hbm, tf_hbm, x_hbm, sf_hbm, pick_hbm, turn_hbm, lw_hbm, w_hbm,
    acc, far_hbm, xo_ref, g1_ref, g2_ref,
    pre_ref, og_ref, tf_ref, x_ref, sf_ref, pick_ref, turn_ref, lw_ref, w_buf, unpick_ref, si_ref, ti_ref,
    slope, gs, gr, xs, xr, ms, mr, ns, nr, bk, bs, br, ts, tr,
    in_sem, tf_sem, far_sem, g_ss, g_rs, x_ss, x_rs, m_ss, m_rs, n_ss, n_rs, b_ss, b_rs, t_ss, t_rs,
):
    nb, rows, c = slope.shape
    _, nk, _, ra, _ = gs.shape
    nq = w_buf.shape[1]
    unit = bk.shape[1] // nq
    pos, mode = lax.axis_index("pos"), lax.axis_index("mode")
    at = {"pos": pos, "mode": mode}
    size = {"pos": np_, "mode": nm}
    peer_of = lambda axis, d: lax.rem(at[axis] + d, size[axis])

    barrier = pltpu.get_barrier_semaphore()
    for axis in ("pos", "mode"):
        for d in range(1, size[axis]):
            pl.semaphore_signal(barrier, inc=1, device_id={axis: peer_of(axis, d)}, device_id_type=MESH)

    far = lax.rem(pos + np_ // 2, np_)
    hbm = (x_hbm, pre_hbm, og_hbm, sf_hbm, pick_hbm, turn_hbm, lw_hbm, w_hbm)
    local = (x_ref, pre_ref, og_ref, sf_ref, pick_ref, turn_ref, lw_ref, w_buf)
    loads = [pltpu.make_async_copy(h, v, in_sem.at[n]) for n, (h, v) in enumerate(zip(hbm, local))]
    tf_loads = [pltpu.make_async_copy(tf_hbm.at[k], tf_ref.at[k], tf_sem.at[k]) for k in range(nk)]
    for load in (loads[0], tf_loads[0], *loads[1:3], *tf_loads[1:], *loads[3:]):
        load.start()
    load_of = {id(v): load for v, load in zip(local, loads)}
    ready = lambda *refs: [load_of[id(r)].wait() for r in refs]

    step = 64

    def slope_step(i):
        b, r = i // (rows // step), pl.multiple_of(i % (rows // step) * step, step)
        values = pre_ref[b, pl.ds(r, step), :].astype(F32)
        cdf = 0.5 * (1.0 + lax.erf(values * 0.7071067811865476))
        density = jnp.exp(-0.5 * values * values) * 0.3989422804014327
        grad = og_ref[b, pl.ds(r, step), :].astype(F32)
        slope[b, pl.ds(r, step), :] = (grad * (cdf + values * density)).astype(BF16)

    def copy(axis, peer, slot, k, src, dst, ss, rs):
        return pltpu.make_async_remote_copy(
            src_ref=src.at[peer, k], dst_ref=dst.at[slot, k], send_sem=ss.at[peer, k], recv_sem=rs.at[slot, k],
            device_id={axis: peer}, device_id_type=MESH,
        )

    def peers(axis, skip, act):
        half = size[axis] // 2
        for first, last in ((1, half), (half + 1, size[axis])) if skip else ((1, size[axis]),):
            if first < last:
                pl.loop(first, last)(lambda d: act(peer_of(axis, d)))

    def send(axis, k, src, dst, ss, rs, skip=False):
        peers(axis, skip, lambda peer: copy(axis, peer, at[axis], k, src, dst, ss, rs).start())
        dst[at[axis], k] = src[at[axis], k]

    def arrive(axis, k, src, dst, ss, rs, skip=False):
        peers(axis, skip, lambda peer: copy(axis, peer, peer, k, src, dst, ss, rs).wait_recv())

    def drain(axis, k, src, dst, ss, rs, skip=False):
        peers(axis, skip, lambda peer: copy(axis, peer, peer, k, src, dst, ss, rs).wait_send())

    g_way = ("pos", gs, gr, g_ss, g_rs)
    x_way = ("pos", xs, xr, x_ss, x_rs)
    m_way = ("mode", ms, mr, m_ss, m_rs)
    n_way = ("mode", ns, nr, n_ss, n_rs)
    b_way = ("mode", bs, br, b_ss, b_rs)
    t_way = ("pos", ts, tr, t_ss, t_rs, True)
    go = lambda act, k, way: act(way[0], k, *way[1:])

    def time_fwd(source, buf, k):
        for b in range(nb):
            buf[:, k, b] = dot(tf_ref[k], source[b]).astype(BF16).reshape(np_, ra, c)

    def space_fwd(source, buf, k, scale):
        res = dot(sf_ref[...], source[:, k].reshape(-1, c))
        if scale != 1.0:
            res = res * scale
        buf[:, k] = res.astype(BF16).reshape(nm, -1, c)

    def gathered(buf, k):
        return buf[:, k].reshape(-1, c)

    ready(x_ref)
    tf_loads[0].wait()
    time_fwd(x_ref, xs, 0)
    pl.semaphore_wait(barrier, np_ - 1 + nm - 1)
    go(send, 0, x_way)
    ready(pre_ref, og_ref)
    pl.loop(0, nb * (rows // step))(slope_step)
    for k in range(nk):
        if k:
            tf_loads[k].wait()
        time_fwd(slope, gs, k)
        go(send, k, g_way)
    for k in range(1, nk):
        time_fwd(x_ref, xs, k)
        go(send, k, x_way)
    tr[far] = jnp.zeros(tr.shape[1:], BF16)
    ready(sf_ref, pick_ref, turn_ref, lw_ref, w_buf)
    unpick_ref[...] = pick_ref[...].T
    si_ref[...] = sf_ref[...].T
    for k in range(nk):
        ti_ref[k] = tf_ref[k].T

    far_copy = lambda k: pltpu.make_async_copy(ts.at[far, k], far_hbm.at[:, k], far_sem.at[k])

    def stage_space(k):
        go(arrive, k, g_way)
        go(drain, k, g_way)
        space_fwd(gr, ms, k, factor)
        go(send, k, m_way)

    def stage_back(k):
        go(arrive, k, m_way)
        field = gathered(mr, k)
        g1_ref[k] = dot(pick_ref[...], field).astype(BF16)
        g2_ref[k] = dot(turn_ref[...], field).astype(BF16)

        @pl.loop(0, nq, unroll=math.gcd(nq, 4))
        def _(q):
            span = pl.ds(pl.multiple_of(q * unit, unit), unit)
            back = dot_t(g1_ref[k, span, :], w_buf[0, q, k]) + dot_t(g2_ref[k, span, :], w_buf[1, q, k])
            bk[k, span, :] = back.astype(BF16)

        bs[:, k] = dot(unpick_ref[...], bk[k]).astype(BF16).reshape(nm, -1, c)
        go(send, k, b_way)

    def stage_spread(k):
        go(arrive, k, b_way)
        spread = dot(si_ref[...], gathered(br, k)).astype(BF16)
        ts[:, k] = spread.reshape(np_, nb, ra, c)
        go(send, k, t_way)
        far_copy(k).start()

    def stage_x(k):
        go(arrive, k, x_way)
        space_fwd(xr, ns, k, 1.0)
        go(send, k, n_way)

    def stage_own(k):
        go(arrive, k, n_way)
        xo_ref[k] = dot(pick_ref[...], gathered(nr, k)).astype(BF16)

    def staged(*stages):
        for n in range(nk + len(stages) - 1):
            for lag, stage in enumerate(stages):
                if 0 <= n - lag < nk:
                    stage(n - lag)

    staged(stage_space, stage_back, stage_spread)
    for b in range(nb):
        acc[b] = dot_t(slope[b], lw_ref[...])
    staged(stage_x, stage_own)
    for k in range(nk):
        for way in (x_way, m_way, n_way, b_way):
            go(drain, k, way)

    for k in range(nk):
        go(arrive, k, t_way)
        for b in range(nb):
            acc[b] = acc[b] + dot(ti_ref[k], tr[:, k, b].reshape(-1, c))
    for k in range(nk):
        go(drain, k, t_way)
        far_copy(k).wait()


def modes_kernel(group, x_ref, g1_ref, g2_ref, out_hbm, buf, sem):
    nk, nq, unit, c = x_ref.shape

    @pl.loop(0, nk)
    def _(k):
        @pl.loop(0, nq // group)
        def _(i):
            first = i * group
            turned = x_ref[k, pl.ds(first, group)].reshape(group * unit, c).T
            for q in range(group):
                for part, g_ref in enumerate((g1_ref, g2_ref)):
                    rows = [jnp.zeros((n * unit, c), BF16) if n else None for n in (q, group - 1 - q)]
                    rows = [v for v in (rows[0], g_ref[k, first + q], rows[1]) if v is not None]
                    field = jnp.concatenate(rows, axis=0) if len(rows) > 1 else rows[0]
                    buf[part, first + q, k] = dot(turned, field).astype(BF16)
                    pltpu.make_async_copy(buf.at[part, first + q, k], out_hbm.at[part, first + q, k], sem).start()

    pltpu.make_async_copy(buf, out_hbm, sem).wait()


def finish_kernel(np_, acc_ref, far_ref, tab_hbm, out_hbm, tab_ref, out_ref, in_sem, out_sem):
    nb = acc_ref.shape[0]
    peer = lax.rem(lax.axis_index("pos") + np_ // 2, np_)
    tab = pltpu.make_async_copy(tab_hbm.at[peer], tab_ref, in_sem)
    outs = [pltpu.make_async_copy(out_ref.at[b], out_hbm.at[b], out_sem.at[b]) for b in range(nb)]
    tab.start()
    tab.wait()
    for b in range(nb):
        out_ref[b] = (acc_ref[b] + dot(tab_ref[...], far_ref[b])).astype(BF16)
        outs[b].start()
    for b in range(nb):
        outs[b].wait()


def on_device(np_, nm, grid_input, preact, out_grad, mode_weight, local_weight):
    nb, na, nt, c = grid_input.shape
    _, nq, nk, _, _ = mode_weight.shape
    factor = 1.0 / (np_ * na * nt)
    consts = tables(np_, nm, nb, na, nt, nk, nq)
    unit = nm * nb * 2
    flat = lambda v: v.reshape(nb, na * nt, c)
    operands = (
        flat(preact), flat(out_grad), consts[0], flat(grid_input), *consts[1:-1], local_weight, mode_weight
    )
    anywhere = pl.BlockSpec(memory_space=pl.ANY)
    on_chip = pl.BlockSpec(memory_space=pltpu.VMEM)
    in_place = pl.BlockSpec(memory_space=pltpu.HBM)
    pos_buf = pltpu.VMEM((np_, nk, nb, 2 * na, c), BF16)
    mode_buf = pltpu.VMEM((nm, nk, nb * 2 * nq, c), BF16)
    owned = jax.ShapeDtypeStruct((nk, nq * unit, c), BF16)
    field = jax.ShapeDtypeStruct((nb, na * nt, c), BF16)
    total = jax.ShapeDtypeStruct(field.shape, F32)
    far = jax.ShapeDtypeStruct((nb, nk, 2 * na, c), BF16)
    dma = pltpu.SemaphoreType.DMA
    sems = [dma((n, nk)) for n in (np_, np_, np_, np_, nm, nm, nm, nm, nm, nm, np_, np_)]
    acc, far, x_own, g1, g2 = pl.pallas_call(
        functools.partial(chain_kernel, np_, nm, factor),
        out_shape=(total, far, owned, owned, owned),
        in_specs=[in_place] * len(operands),
        out_specs=(on_chip, anywhere, on_chip, on_chip, on_chip),
        scratch_shapes=[pltpu.VMEM(v.shape, BF16) for v in operands]
        + [
            pltpu.VMEM(consts[2].shape, BF16),
            pltpu.VMEM(consts[1].shape[::-1], BF16),
            pltpu.VMEM((nk, na * nt, np_ * 2 * na), BF16),
            pltpu.VMEM(field.shape, BF16),
            pos_buf, pos_buf, pos_buf, pos_buf,
            mode_buf, mode_buf, mode_buf, mode_buf,
            pltpu.VMEM(owned.shape, BF16),
            mode_buf, mode_buf,
            pos_buf, pos_buf,
            dma((len(operands),)), dma((nk,)), dma((nk,)),
        ] + sems,
        compiler_params=pltpu.CompilerParams(
            collective_id=0, has_side_effects=True, vmem_limit_bytes=40 * 1024 * 1024
        ),
        name="chain",
    )(*[pltpu.with_memory_space_constraint(v, pltpu.HBM) for v in operands])

    far = lax.ppermute(far, "pos", [(n, (n + np_ // 2) % np_) for n in range(np_)])
    per_q = lambda v: v.reshape(nk, nq, unit, c)
    group = max(n for n in range(1, nq + 1) if nq % n == 0 and n * unit <= max(GROUP, unit))
    grad_modes = pl.pallas_call(
        functools.partial(modes_kernel, group),
        out_shape=jax.ShapeDtypeStruct(mode_weight.shape, BF16),
        in_specs=[on_chip] * 3,
        out_specs=anywhere,
        scratch_shapes=[pltpu.VMEM(mode_weight.shape, BF16), dma(())],
        cost_estimate=pl.CostEstimate(
            flops=2 * unit * mode_weight.size, bytes_accessed=2 * mode_weight.size, transcendentals=0
        ),
        compiler_params=pltpu.CompilerParams(vmem_limit_bytes=24 * 1024 * 1024),
        name="modes",
    )(per_q(x_own), per_q(g1), per_q(g2))
    grad_input = pl.pallas_call(
        functools.partial(finish_kernel, np_),
        out_shape=field,
        in_specs=[on_chip, on_chip, in_place],
        out_specs=anywhere,
        scratch_shapes=[
            pltpu.VMEM(consts[-1].shape[1:], BF16),
            pltpu.VMEM(field.shape, BF16),
            dma(()), dma((nb,)),
        ],
        compiler_params=pltpu.CompilerParams(vmem_limit_bytes=16 * 1024 * 1024),
        name="finish",
    )(acc, far.reshape(nb, nk * 2 * na, c), consts[-1])
    return (grad_input.reshape(grid_input.shape), grad_modes)


def solution(mesh):
    return jax.shard_map(
        functools.partial(on_device, mesh.shape["pos"], mesh.shape["mode"]),
        mesh=mesh,
        in_specs=(
            P("mode", "pos", None, None),
            P("mode", "pos", None, None),
            P("mode", "pos", None, None),
            P(None, "mode", "pos", None, None),
            P(),
        ),
        out_specs=(P("mode", "pos", None, None), P(None, "mode", "pos", None, None)),
        check_vma=False,
    )
```

```python
import functools
import math

import jax
import jax.numpy as jnp
import ml_dtypes
import numpy as np
from jax import lax
from jax.experimental import pallas as pl
from jax.experimental.pallas import tpu as pltpu
from jax.sharding import PartitionSpec as P

MESH = pl.DeviceIdType.MESH
F32 = jnp.float32
BF16 = jnp.bfloat16
GROUP = 128


def twiddle(length, mode_count):
    angles = (np.arange(length)[:, None] * np.arange(mode_count)[None, :] % length) * (2.0 * math.pi / length)
    as_bf16 = lambda v: v.astype(np.float32).astype(ml_dtypes.bfloat16).astype(np.float32)
    return as_bf16(np.cos(angles)), as_bf16(np.sin(angles))


def tables(np_, nm, nb, na, nt, nk, nq):
    cos_t, sin_t = twiddle(nt, np_ * nk)
    cos_s, sin_s = twiddle(np_ * na, nm * nq)
    eye_a, eye_b, eye_m, eye_q = np.eye(na), np.eye(nb), np.eye(nm), np.eye(nq)
    out = lambda v, *shape: jnp.asarray(v.reshape(shape).astype(ml_dtypes.bfloat16))
    by_k = np.stack([cos_t, -sin_t])
    by_k = by_k.reshape(2, nt, np_, nk)
    time_fwd = np.einsum("rtpk,ab->kprabt", by_k, eye_a)
    time_far = np.einsum("rtpk,ab->patkrb", by_k, eye_a)
    fwd = np.stack([np.stack([cos_s, sin_s]), np.stack([-sin_s, cos_s])])
    fwd = fwd.reshape(2, 2, np_, na, nm, nq)
    space_fwd = np.einsum("rspamq,bc->mbrqpcsa", fwd, eye_b)
    pick = np.einsum("rs,qu,mn,bc->qrmbncsu", np.eye(2), eye_q, eye_m, eye_b)
    turn = np.einsum("rs,qu,mn,bc->qrmbncsu", np.array([[0.0, 1.0], [-1.0, 0.0]]), eye_q, eye_m, eye_b)
    rows = nm * nb * 2 * nq
    return (
        out(time_fwd, nk, np_ * 2 * na, na * nt),
        out(space_fwd, rows, np_ * nb * 2 * na),
        out(pick, rows, rows),
        out(turn, rows, rows),
        out(time_far, np_, na * nt, nk * 2 * na),
    )


def dot(a, b):
    return jnp.dot(a, b, preferred_element_type=F32)


def dot_t(a, b):
    return lax.dot_general(a, b, (((1,), (1,)), ((), ())), preferred_element_type=F32)


def chain_kernel(
    np_, nm, factor,
    pre_hbm, og_hbm, tf_hbm, x_hbm, sf_hbm, pick_hbm, turn_hbm, lw_hbm, w_hbm,
    acc, far_hbm, xo_ref, g1_ref, g2_ref,
    pre_ref, og_ref, tf_ref, x_ref, sf_ref, pick_ref, turn_ref, lw_ref, w_buf, unpick_ref, si_ref, ti_ref,
    slope, gs, gr, xs, xr, ms, mr, ns, nr, bk, bs, br, ts, tr,
    in_sem, tf_sem, far_sem, g_ss, g_rs, x_ss, x_rs, m_ss, m_rs, n_ss, n_rs, b_ss, b_rs, t_ss, t_rs,
):
    nb, rows, c = slope.shape
    _, nk, _, ra, _ = gs.shape
    nq = w_buf.shape[1]
    unit = bk.shape[1] // nq
    pos, mode = lax.axis_index("pos"), lax.axis_index("mode")
    at = {"pos": pos, "mode": mode}
    size = {"pos": np_, "mode": nm}
    peer_of = lambda axis, d: lax.rem(at[axis] + d, size[axis])

    barrier = pltpu.get_barrier_semaphore()
    for axis in ("pos", "mode"):
        for d in range(1, size[axis]):
            pl.semaphore_signal(barrier, inc=1, device_id={axis: peer_of(axis, d)}, device_id_type=MESH)

    far = lax.rem(pos + np_ // 2, np_)
    hbm = (x_hbm, pre_hbm, og_hbm, sf_hbm, pick_hbm, turn_hbm, lw_hbm, w_hbm)
    local = (x_ref, pre_ref, og_ref, sf_ref, pick_ref, turn_ref, lw_ref, w_buf)
    loads = [pltpu.make_async_copy(h, v, in_sem.at[n]) for n, (h, v) in enumerate(zip(hbm, local))]
    tf_loads = [pltpu.make_async_copy(tf_hbm.at[k], tf_ref.at[k], tf_sem.at[k]) for k in range(nk)]
    for load in (loads[0], tf_loads[0], *loads[1:3], *tf_loads[1:], *loads[3:]):
        load.start()
    load_of = {id(v): load for v, load in zip(local, loads)}
    ready = lambda *refs: [load_of[id(r)].wait() for r in refs]

    step = 64

    def slope_step(i):
        b, r = i // (rows // step), pl.multiple_of(i % (rows // step) * step, step)
        values = pre_ref[b, pl.ds(r, step), :].astype(F32)
        cdf = 0.5 * (1.0 + lax.erf(values * 0.7071067811865476))
        density = jnp.exp(-0.5 * values * values) * 0.3989422804014327
        grad = og_ref[b, pl.ds(r, step), :].astype(F32)
        slope[b, pl.ds(r, step), :] = (grad * (cdf + values * density)).astype(BF16)

    def copy(axis, peer, slot, k, src, dst, ss, rs):
        return pltpu.make_async_remote_copy(
            src_ref=src.at[peer, k], dst_ref=dst.at[slot, k], send_sem=ss.at[peer, k], recv_sem=rs.at[slot, k],
            device_id={axis: peer}, device_id_type=MESH,
        )

    def peers(axis, skip, act):
        half = size[axis] // 2
        for first, last in ((1, half), (half + 1, size[axis])) if skip else ((1, size[axis]),):
            if first < last:
                pl.loop(first, last)(lambda d: act(peer_of(axis, d)))

    def send(axis, k, src, dst, ss, rs, skip=False):
        if skip and size[axis] % 4 == 0:
            quarter = size[axis] // 4

            @pl.loop(0, size[axis])
            def _(i):
                block = i // quarter
                base = jnp.where(block < 2, block * 2, block * 2 - 3) * quarter
                peer = base + lax.rem(i + at[axis], quarter)
                there = jnp.logical_and(peer != at[axis], peer != lax.rem(at[axis] + size[axis] // 2, size[axis]))

                @pl.when(there)
                def _():
                    copy(axis, peer, at[axis], k, src, dst, ss, rs).start()
        else:
            peers(axis, skip, lambda peer: copy(axis, peer, at[axis], k, src, dst, ss, rs).start())
        dst[at[axis], k] = src[at[axis], k]

    def arrive(axis, k, src, dst, ss, rs, skip=False):
        peers(axis, skip, lambda peer: copy(axis, peer, peer, k, src, dst, ss, rs).wait_recv())

    def drain(axis, k, src, dst, ss, rs, skip=False):
        peers(axis, skip, lambda peer: copy(axis, peer, peer, k, src, dst, ss, rs).wait_send())

    g_way = ("pos", gs, gr, g_ss, g_rs)
    x_way = ("pos", xs, xr, x_ss, x_rs)
    m_way = ("mode", ms, mr, m_ss, m_rs)
    n_way = ("mode", ns, nr, n_ss, n_rs)
    b_way = ("mode", bs, br, b_ss, b_rs)
    t_way = ("pos", ts, tr, t_ss, t_rs, True)
    go = lambda act, k, way: act(way[0], k, *way[1:])

    def time_fwd(source, buf, k):
        for b in range(nb):
            buf[:, k, b] = dot(tf_ref[k], source[b]).astype(BF16).reshape(np_, ra, c)

    def space_fwd(source, buf, k, scale):
        res = dot(sf_ref[...], source[:, k].reshape(-1, c))
        if scale != 1.0:
            res = res * scale
        buf[:, k] = res.astype(BF16).reshape(nm, -1, c)

    def gathered(buf, k):
        return buf[:, k].reshape(-1, c)

    ready(x_ref)
    tf_loads[0].wait()
    time_fwd(x_ref, xs, 0)
    pl.semaphore_wait(barrier, np_ - 1 + nm - 1)
    go(send, 0, x_way)
    ready(pre_ref, og_ref)
    pl.loop(0, nb * (rows // step))(slope_step)
    for k in range(nk):
        if k:
            tf_loads[k].wait()
        time_fwd(slope, gs, k)
        go(send, k, g_way)
    for k in range(1, nk):
        time_fwd(x_ref, xs, k)
        go(send, k, x_way)
    tr[far] = jnp.zeros(tr.shape[1:], BF16)
    ready(sf_ref, pick_ref, turn_ref, lw_ref, w_buf)
    unpick_ref[...] = pick_ref[...].T
    si_ref[...] = sf_ref[...].T
    for k in range(nk):
        ti_ref[k] = tf_ref[k].T

    far_copy = lambda k: pltpu.make_async_copy(ts.at[far, k], far_hbm.at[:, k], far_sem.at[k])

    def stage_space(k):
        go(arrive, k, g_way)
        go(drain, k, g_way)
        space_fwd(gr, ms, k, factor)
        go(send, k, m_way)

    def stage_back(k):
        go(arrive, k, m_way)
        field = gathered(mr, k)
        g1_ref[k] = dot(pick_ref[...], field).astype(BF16)
        g2_ref[k] = dot(turn_ref[...], field).astype(BF16)

        @pl.loop(0, nq, unroll=math.gcd(nq, 4))
        def _(q):
            span = pl.ds(pl.multiple_of(q * unit, unit), unit)
            back = dot_t(g1_ref[k, span, :], w_buf[0, q, k]) + dot_t(g2_ref[k, span, :], w_buf[1, q, k])
            bk[k, span, :] = back.astype(BF16)

        bs[:, k] = dot(unpick_ref[...], bk[k]).astype(BF16).reshape(nm, -1, c)
        go(send, k, b_way)

    def stage_spread(k):
        go(arrive, k, b_way)
        spread = dot(si_ref[...], gathered(br, k)).astype(BF16)
        ts[:, k] = spread.reshape(np_, nb, ra, c)
        go(send, k, t_way)
        far_copy(k).start()

    def stage_x(k):
        go(arrive, k, x_way)
        space_fwd(xr, ns, k, 1.0)
        go(send, k, n_way)

    def stage_own(k):
        go(arrive, k, n_way)
        xo_ref[k] = dot(pick_ref[...], gathered(nr, k)).astype(BF16)

    def staged(*stages):
        for n in range(nk + len(stages) - 1):
            for lag, stage in enumerate(stages):
                if 0 <= n - lag < nk:
                    stage(n - lag)

    staged(stage_space, stage_back, stage_spread)
    for b in range(nb):
        acc[b] = dot_t(slope[b], lw_ref[...])
    staged(stage_x, stage_own)
    for k in range(nk):
        for way in (x_way, m_way, n_way, b_way):
            go(drain, k, way)

    for k in range(nk):
        go(arrive, k, t_way)
        for b in range(nb):
            acc[b] = acc[b] + dot(ti_ref[k], tr[:, k, b].reshape(-1, c))
    for k in range(nk):
        go(drain, k, t_way)
        far_copy(k).wait()


def modes_kernel(group, x_ref, g1_ref, g2_ref, out_hbm, buf, sem):
    nk, nq, unit, c = x_ref.shape

    @pl.loop(0, nk)
    def _(k):
        @pl.loop(0, nq // group)
        def _(i):
            first = i * group
            turned = x_ref[k, pl.ds(first, group)].reshape(group * unit, c).T
            for q in range(group):
                for part, g_ref in enumerate((g1_ref, g2_ref)):
                    rows = [jnp.zeros((n * unit, c), BF16) if n else None for n in (q, group - 1 - q)]
                    rows = [v for v in (rows[0], g_ref[k, first + q], rows[1]) if v is not None]
                    field = jnp.concatenate(rows, axis=0) if len(rows) > 1 else rows[0]
                    buf[part, first + q, k] = dot(turned, field).astype(BF16)
                    pltpu.make_async_copy(buf.at[part, first + q, k], out_hbm.at[part, first + q, k], sem).start()

    pltpu.make_async_copy(buf, out_hbm, sem).wait()


def finish_kernel(np_, acc_ref, far_ref, tab_hbm, out_hbm, tab_ref, out_ref, in_sem, out_sem):
    nb = acc_ref.shape[0]
    peer = lax.rem(lax.axis_index("pos") + np_ // 2, np_)
    tab = pltpu.make_async_copy(tab_hbm.at[peer], tab_ref, in_sem)
    outs = [pltpu.make_async_copy(out_ref.at[b], out_hbm.at[b], out_sem.at[b]) for b in range(nb)]
    tab.start()
    tab.wait()
    for b in range(nb):
        out_ref[b] = (acc_ref[b] + dot(tab_ref[...], far_ref[b])).astype(BF16)
        outs[b].start()
    for b in range(nb):
        outs[b].wait()


def on_device(np_, nm, grid_input, preact, out_grad, mode_weight, local_weight):
    nb, na, nt, c = grid_input.shape
    _, nq, nk, _, _ = mode_weight.shape
    factor = 1.0 / (np_ * na * nt)
    consts = tables(np_, nm, nb, na, nt, nk, nq)
    unit = nm * nb * 2
    flat = lambda v: v.reshape(nb, na * nt, c)
    operands = (
        flat(preact), flat(out_grad), consts[0], flat(grid_input), *consts[1:-1], local_weight, mode_weight
    )
    anywhere = pl.BlockSpec(memory_space=pl.ANY)
    on_chip = pl.BlockSpec(memory_space=pltpu.VMEM)
    in_place = pl.BlockSpec(memory_space=pltpu.HBM)
    pos_buf = pltpu.VMEM((np_, nk, nb, 2 * na, c), BF16)
    mode_buf = pltpu.VMEM((nm, nk, nb * 2 * nq, c), BF16)
    owned = jax.ShapeDtypeStruct((nk, nq * unit, c), BF16)
    field = jax.ShapeDtypeStruct((nb, na * nt, c), BF16)
    total = jax.ShapeDtypeStruct(field.shape, F32)
    far = jax.ShapeDtypeStruct((nb, nk, 2 * na, c), BF16)
    dma = pltpu.SemaphoreType.DMA
    sems = [dma((n, nk)) for n in (np_, np_, np_, np_, nm, nm, nm, nm, nm, nm, np_, np_)]
    acc, far, x_own, g1, g2 = pl.pallas_call(
        functools.partial(chain_kernel, np_, nm, factor),
        out_shape=(total, far, owned, owned, owned),
        in_specs=[in_place] * len(operands),
        out_specs=(on_chip, anywhere, on_chip, on_chip, on_chip),
        scratch_shapes=[pltpu.VMEM(v.shape, BF16) for v in operands]
        + [
            pltpu.VMEM(consts[2].shape, BF16),
            pltpu.VMEM(consts[1].shape[::-1], BF16),
            pltpu.VMEM((nk, na * nt, np_ * 2 * na), BF16),
            pltpu.VMEM(field.shape, BF16),
            pos_buf, pos_buf, pos_buf, pos_buf,
            mode_buf, mode_buf, mode_buf, mode_buf,
            pltpu.VMEM(owned.shape, BF16),
            mode_buf, mode_buf,
            pos_buf, pos_buf,
            dma((len(operands),)), dma((nk,)), dma((nk,)),
        ] + sems,
        compiler_params=pltpu.CompilerParams(
            collective_id=0, has_side_effects=True, vmem_limit_bytes=40 * 1024 * 1024
        ),
        name="chain",
    )(*[pltpu.with_memory_space_constraint(v, pltpu.HBM) for v in operands])

    far = lax.ppermute(far, "pos", [(n, (n + np_ // 2) % np_) for n in range(np_)])
    per_q = lambda v: v.reshape(nk, nq, unit, c)
    group = max(n for n in range(1, nq + 1) if nq % n == 0 and n * unit <= max(GROUP, unit))
    grad_modes = pl.pallas_call(
        functools.partial(modes_kernel, group),
        out_shape=jax.ShapeDtypeStruct(mode_weight.shape, BF16),
        in_specs=[on_chip] * 3,
        out_specs=anywhere,
        scratch_shapes=[pltpu.VMEM(mode_weight.shape, BF16), dma(())],
        cost_estimate=pl.CostEstimate(
            flops=2 * unit * mode_weight.size, bytes_accessed=2 * mode_weight.size, transcendentals=0
        ),
        compiler_params=pltpu.CompilerParams(vmem_limit_bytes=24 * 1024 * 1024),
        name="modes",
    )(per_q(x_own), per_q(g1), per_q(g2))
    grad_input = pl.pallas_call(
        functools.partial(finish_kernel, np_),
        out_shape=field,
        in_specs=[on_chip, on_chip, in_place],
        out_specs=anywhere,
        scratch_shapes=[
            pltpu.VMEM(consts[-1].shape[1:], BF16),
            pltpu.VMEM(field.shape, BF16),
            dma(()), dma((nb,)),
        ],
        compiler_params=pltpu.CompilerParams(vmem_limit_bytes=16 * 1024 * 1024),
        name="finish",
    )(acc, far.reshape(nb, nk * 2 * na, c), consts[-1])
    return (grad_input.reshape(grid_input.shape), grad_modes)


def solution(mesh):
    return jax.shard_map(
        functools.partial(on_device, mesh.shape["pos"], mesh.shape["mode"]),
        mesh=mesh,
        in_specs=(
            P("mode", "pos", None, None),
            P("mode", "pos", None, None),
            P("mode", "pos", None, None),
            P(None, "mode", "pos", None, None),
            P(),
        ),
        out_specs=(P("mode", "pos", None, None), P(None, "mode", "pos", None, None)),
        check_vma=False,
    )
```
